512 devices in a mesh: gx: 16 (over y, core), gy: 32 (over z, x).
Axes of the slice: x: 4, y: 8, z: 8, core: 2. Of those that a mesh axis runs over, the one named last changes fastest.
Arguments:
- tensor: float32 [4096, 4096, 8], P('gx', 'gy'), may hold values from -6 to 6
- sketch_one: float32 [4096, 8, 256], P('gy'), may hold values from -0.03125 to 0.03125
- sketch_two: float32 [256, 8, 256], P('gx'), may hold values from -0.125 to 0.125
Outputs:
- basis_one: float32 [4096, 256], P('gx')
- basis_two: float32 [4096, 256], P('gy')
- core: float32 [256, 256, 8], P('gx', 'gy')
The draws below stay inside these ranges and needn't reach their ends.
All inputs are finite; a program needn't handle non-finite values.
Results may differ from the reference program's by a relative error of at most 0.00008.
Values sent between devices are 32-bit elements; how exact they have to be, the bound alone decides.
No kernel may reach another device: no remote copies, remote signals or barrier semaphores. Data moves between devices by JAX's collectives and lax.ppermute only.
A program may use at most 64 MiB of HBM per device.

```python
import jax
import jax.numpy as jnp
from jax import lax

S = 256
K3 = 8
N1 = 4096
N2 = 4096


def shard_levels(stream_key, dims, split, least, high):
    gain = 1.0
    for position, parts in split:
        steps = jax.random.uniform(jax.random.fold_in(jax.random.fold_in(stream_key, 6), position), (parts,), jnp.float32, least / len(split), high / len(split))
        gain = gain * jnp.repeat(jnp.exp(steps), dims[position] // parts).reshape((-1,) + (1,) * (len(dims) - 1 - position))
    return gain


def gaussian(rng, extent, scale, most, pieces=(), kind=jnp.bfloat16):
    factor_of = shard_levels(rng, extent, pieces, -0.22, 0.18) if pieces else 1.0
    entries = jax.random.normal(rng, extent, jnp.float32) * scale * factor_of
    return jnp.minimum(jnp.maximum(entries, -most), most).astype(kind)


def setup_inputs(seed: int = 0) -> dict:
    seeds = jax.random.split(jax.random.key(seed), 4)
    tensor = gaussian(seeds[0], (N1, N2, K3), 1.0, 6.0, ((0, 16), (1, 32)), jnp.float32)
    sketch_one = gaussian(seeds[1], (N2, K3, S), (N2 * K3) ** -0.5, 0.03125, ((0, 32),), jnp.float32)
    sketch_two = gaussian(seeds[2], (S, K3, S), (S * K3) ** -0.5, 0.125, ((0, 16),), jnp.float32)
    return dict(tensor=tensor, sketch_one=sketch_one, sketch_two=sketch_two)


def orthonormal(matrix):
    gram_total = jnp.dot(matrix.T, matrix, precision=lax.Precision.HIGHEST)
    factor = jnp.linalg.cholesky(gram_total)
    return lax.linalg.triangular_solve(factor, matrix, left_side=False, lower=True, transpose_a=True)

def reference(tensor, sketch_one, sketch_two):
    unfolded = tensor.reshape(N1, N2 * K3)
    first_sketch = jnp.dot(unfolded, sketch_one.reshape(N2 * K3, S), precision=lax.Precision.HIGHEST)
    basis_one = orthonormal(first_sketch)
    partial_core = jnp.dot(basis_one.T, unfolded, precision=lax.Precision.HIGHEST).reshape(S, N2, K3)
    second_sketch = jnp.einsum('rjk,rkc->jc', partial_core, sketch_two, precision=lax.Precision.HIGHEST)
    basis_two = orthonormal(second_sketch)
    core = jnp.einsum('rjk,js->rsk', partial_core, basis_two, precision=lax.Precision.HIGHEST)
    return (basis_one, basis_two, core)
```

```python
import jax
import jax.numpy as jnp
from jax import lax
from jax.sharding import PartitionSpec as P

HI = lax.Precision.HIGHEST


def swap(pieces, axis):
    return lax.all_to_all(pieces, axis, 0, 0, tiled=True)


def sum_scatter(total, axis):
    parts = lax.axis_size(axis)
    pieces = total.reshape((parts, total.shape[0] // parts) + total.shape[1:])
    return swap(pieces, axis).sum(0)


def gather(piece, axis):
    parts = lax.axis_size(axis)
    got = swap(jnp.broadcast_to(piece[None], (parts,) + piece.shape), axis)
    return got.reshape((parts * piece.shape[0],) + piece.shape[1:])


def inverse_factor(gram):
    factor = jnp.linalg.cholesky(gram)
    eye = jnp.eye(gram.shape[0], dtype=gram.dtype)
    return lax.linalg.triangular_solve(factor, eye, left_side=False, lower=True, transpose_a=True)


def local(tensor, sketch_one, sketch_two):
    rows_one, rows_two, depth = tensor.shape
    width = sketch_one.shape[2]
    gx, gy = lax.axis_size("gx"), lax.axis_size("gy")
    cells = rows_two // gx
    rank_rows = width // gx
    cols = width // gy

    sketch_all = gather(sketch_two, "gx")

    part = jnp.einsum("ijk,jkc->ic", tensor, sketch_one, precision=HI)
    first = gather(sum_scatter(part, "gy"), "gy")

    gram_part = lax.dot_general(first, first, (((0,), (0,)), ((), ())), precision=HI)
    gram = gather(sum_scatter(gram_part, "gx"), "gx")
    mixed_part = jnp.einsum("ijk,ir->jkr", tensor, first, precision=HI)
    mixed_part, gram = lax.optimization_barrier((mixed_part, gram))
    mixed = sum_scatter(mixed_part, "gx")

    inv_one = inverse_factor(gram)
    basis_one = jnp.dot(first, inv_one, precision=HI)
    core_t = jnp.einsum("jkr,rs->jks", mixed, inv_one, precision=HI)
    second_own = jnp.einsum("jks,skc->jc", core_t, sketch_all, precision=HI)

    share = jnp.transpose(core_t.reshape(cells, depth, gx, rank_rows), (2, 0, 3, 1))
    share = share.reshape(gx, cells * rank_rows * depth // width, width)
    own = jnp.broadcast_to(second_own[None], (gx, cells, width))
    got = swap(jnp.concatenate([own, share], axis=1), "gx")
    second = got[:, :cells].reshape(rows_two, width)
    core_rows = got[:, cells:].reshape(rows_two, rank_rows * depth)

    left = jnp.concatenate([second, core_rows], axis=1)
    both_part = lax.dot_general(left, second, (((0,), (0,)), ((), ())), precision=HI)
    both = gather(sum_scatter(both_part, "gy"), "gy")
    inv_two = inverse_factor(both[:width])
    basis_two = jnp.dot(second, inv_two, precision=HI)
    mine = lax.dynamic_slice_in_dim(inv_two, lax.axis_index("gy") * cols, cols, 1)
    core = jnp.dot(both[width:], mine, precision=HI).reshape(rank_rows, depth, cols)
    return (basis_one, basis_two, jnp.swapaxes(core, 1, 2))


def solution(mesh):
    in_specs = (P("gx", "gy", None), P("gy", None, None), P("gx", None, None))
    out_specs = (P("gx", None), P("gy", None), P("gx", "gy", None))
    return jax.shard_map(local, mesh=mesh, in_specs=in_specs, out_specs=out_specs, check_vma=False)
```

```python
import jax
import jax.numpy as jnp
from jax import lax
from jax.experimental import pallas as pl
from jax.experimental.pallas import tpu as pltpu
from jax.sharding import PartitionSpec as P

HI = lax.Precision.HIGHEST
H = 128


def spread_col(x,p):
    return jnp.broadcast_to(x[:,p:p+1],(8,H))


def spread_row(x,r):
    return jnp.broadcast_to(x[r:r+1,:],(8,H))


def eliminate(d_ref,e_ref,x_ref):
    sub=lax.broadcasted_iota(jnp.int32,(8,H),0)
    lane=lax.broadcasted_iota(jnp.int32,(8,H),1)
    for k in range(16):
        rows=slice(8*k,8*k+8)
        block=(lane>=8*k)&(lane<8*k+8)
        Dk=d_ref[rows,:]; Ek=e_ref[rows,:]
        cb=[spread_col(Dk,8*k+t) for t in range(8)]
        s=[[spread_row(cb[t],q) for t in range(q+1)] for q in range(8)]
        Dm=jnp.where(block,jnp.where(lane==8*k+sub,1.0,0.0),Dk)
        rD=[spread_row(Dm,t) for t in range(8)]
        rE=[spread_row(Ek,t) for t in range(8)]
        inv=[None]*8; f=[[None]*8 for _ in range(8)]; W=[[None]*8 for _ in range(8)]
        dsel=s[0][0]
        for j in range(8):
            inv[j]=1.0/s[j][j]
            if j: dsel=jnp.where(sub==j,s[j][j],dsel)
            for q in range(j+1,8):
                f[q][j]=s[q][j]*inv[j]
            for q in range(j+1,8):
                for t in range(j+1,q+1):
                    s[q][t]=s[q][t]-f[q][j]*s[t][j]
        for q in range(8):
            for t in range(q):
                a=f[q][t]
                for m in range(t+1,q):
                    a=a+f[q][m]*W[m][t]
                W[q][t]=-a
        uD=list(rD); uE=list(rE)
        for q in range(1,8):
            for t in range(q):
                uD[q]=uD[q]+W[q][t]*rD[t]
                uE[q]=uE[q]+W[q][t]*rE[t]
        for g in range(k+1,16):
            gr=slice(8*g,8*g+8)
            Dg=d_ref[gr,:]; Eg=e_ref[gr,:]
            c=[spread_col(Dg,8*k+t) for t in range(8)]
            Dg=jnp.where(block,0.0,Dg)
            for j in range(8):
                a=c[j]
                for t in range(j):
                    a=a+W[j][t]*c[t]
                a=a*inv[j]
                Dg=Dg-a*uD[j]; Eg=Eg-a*uE[j]
            d_ref[gr,:]=Dg; e_ref[gr,:]=Eg
        rs=1.0/jnp.sqrt(dsel)
        nD=uD[0]; nE=uE[0]
        for q in range(1,8):
            nD=jnp.where(sub==q,uD[q],nD); nE=jnp.where(sub==q,uE[q],nE)
        row=8*k+sub
        x_ref[rows,:]=jnp.where(lane<=row,nD,0.0)*rs
        e_ref[rows,:]=nE*rs


def dot0(a,b):
    return lax.dot_general(a,b,(((0,),(0,)),((),())),precision=HI,preferred_element_type=jnp.float32)


def dot_t(a, b):
    return lax.dot_general(a, b, (((1,), (1,)), ((), ())), precision=HI, preferred_element_type=jnp.float32)


def factor_rows(g_ref, o_ref, d_ref, e_ref, x_ref):
    d_ref[...] = g_ref[:H, :H]
    e_ref[...] = g_ref[:H, H:]

    def body(b, carry):
        eliminate(d_ref, e_ref, x_ref)

        @pl.when(b == 0)
        def _():
            o_ref[:H, :H] = x_ref[...]
            o_ref[:H, H:] = jnp.zeros((H, H), jnp.float32)
            u = e_ref[...]
            d_ref[...] = g_ref[H:, H:] - dot0(u, u)
            e_ref[...] = -dot0(u, x_ref[...])

        return carry

    lax.fori_loop(0, 2, body, 0)
    o_ref[H:, H:] = x_ref[...]
    o_ref[H:, :H] = e_ref[...]


def first_factor_kernel(i_ref, g_ref, o_ref, p_ref, d_ref, e_ref, x_ref):
    factor_rows(g_ref, o_ref, d_ref, e_ref, x_ref)
    me = i_ref[0]
    y, c = me >> 1, me & 1
    for b in range(16):
        their_y, their_c = b // 2, b % 2
        step = (y - their_y) if their_c == 0 else (their_y - y)
        place = 8 * (c ^ their_c) + (step & 7)
        p_ref[pl.ds(pl.multiple_of(16 * place, 16), 16), :] = o_ref[16 * b : 16 * b + 16, :]


def second_factor_kernel(g_ref, left_ref, o_ref, b_ref, d_ref, e_ref, x_ref):
    factor_rows(g_ref, o_ref, d_ref, e_ref, x_ref)
    b_ref[...] = dot_t(left_ref[:, :256], o_ref[...])


def second_sketch_kernel(m_ref, x_ref, p_ref, s_ref, t_ref, o_ref):
    mixed = m_ref[0]
    for i in range(1, 8):
        mixed = mixed + m_ref[i]
    placed = dot_t(mixed, p_ref[...])
    second = jnp.zeros((8, 256), jnp.float32)
    for k in range(8):
        rows = placed[8 * k : 8 * k + 8]
        for half, ref in enumerate((s_ref, t_ref)):
            block = ref[:, k].reshape(H, 256)
            second = second + jnp.dot(
                rows[:, H * half : H * half + H], block, precision=HI, preferred_element_type=jnp.float32
            )
    core = dot_t(mixed, x_ref[...])
    lane = lax.broadcasted_iota(jnp.int32, (8, H), 1)
    for m in range(16):
        chunk = jnp.zeros((8, H), jnp.float32)
        for k in range(8):
            half = core[8 * k : 8 * k + 8, H * (m // 8) : H * (m // 8) + H]
            shift = (16 * (k - m % 8)) % H
            moved = pltpu.roll(half, shift, 1) if shift else half
            chunk = jnp.where((lane >= 16 * k) & (lane < 16 * k + 16), moved, chunk)
        o_ref[m, :, :256] = second
        o_ref[m, :, 256:] = chunk


VMEM = pl.BlockSpec(memory_space=pltpu.VMEM)
SMEM = pl.BlockSpec(memory_space=pltpu.SMEM)
SQUARE = jax.ShapeDtypeStruct((256, 256), jnp.float32)
SCRATCH = [pltpu.VMEM((H, H), jnp.float32)] * 3
FACTOR_COST = pl.CostEstimate(flops=6_000_000_000, bytes_accessed=786432, transcendentals=0)


def first_factor(index, gram):
    return pl.pallas_call(
        first_factor_kernel,
        out_shape=(SQUARE, SQUARE),
        in_specs=[SMEM, VMEM],
        out_specs=(VMEM, VMEM),
        scratch_shapes=SCRATCH,
        cost_estimate=FACTOR_COST,
        name="first_factor",
    )(index, gram)


def second_factor(gram, left):
    return pl.pallas_call(
        second_factor_kernel,
        out_shape=(SQUARE, jax.ShapeDtypeStruct((128, 256), jnp.float32)),
        in_specs=[VMEM, VMEM],
        out_specs=(VMEM, VMEM),
        scratch_shapes=SCRATCH,
        cost_estimate=FACTOR_COST,
        name="second_factor",
    )(gram, left)


def second_sketch(mixed, inverse, placed, near, far):
    return pl.pallas_call(
        second_sketch_kernel,
        out_shape=jax.ShapeDtypeStruct((16, 8, 384), jnp.float32),
        in_specs=[VMEM] * 5,
        out_specs=VMEM,
        cost_estimate=pl.CostEstimate(flops=200_000_000, bytes_accessed=4_000_000, transcendentals=0),
        name="second_sketch",
    )(mixed, inverse, placed, near, far)


def swap(pieces, axis, groups=None):
    return lax.all_to_all(pieces, axis, 0, 0, axis_index_groups=groups, tiled=True)


def sum_scatter(pieces, axis):
    return swap(pieces, axis).sum(0)


def spread(piece, axis):
    return swap(jnp.broadcast_to(piece[None], (lax.axis_size(axis),) + piece.shape), axis)


def local(tensor, sketch_one, sketch_two):
    gx, gy = 16, 32
    row, col = lax.axis_index("gx"), lax.axis_index("gy")
    core_of = row % 2
    twin = [(i, i ^ 1) for i in range(gx)]

    def turn(d):
        return [(2 * y + c, 2 * ((y + (d if c == 0 else -d)) % 8) + c) for y in range(8) for c in range(2)]

    near = jnp.swapaxes(sketch_two, 0, 1)[None]
    for d in (1, 2, 4):
        near = jnp.concatenate([near, lax.ppermute(near, "gx", turn(d))], axis=0)
    far = lax.ppermute(near, "gx", twin)

    part = jnp.einsum("ijk,jkc->ic", tensor, sketch_one, precision=HI)
    first_own = sum_scatter(part.reshape(gy, 8, 256), "gy")
    first = spread(first_own, "gy").reshape(256, 256)

    gram_part = lax.dot_general(first, first, (((0,), (0,)), ((), ())), precision=HI)
    gram_own = spread(lax.dynamic_slice_in_dim(gram_part, 8 * col, 8, 0), "gx").sum(0)
    gram = spread(gram_own, "gy").reshape(256, 256)

    mixed_part = jnp.einsum("ijk,ir->kjr", tensor, first, precision=HI)
    mixed_part = mixed_part.reshape(8, 8, 2, 8, 256).transpose(2, 1, 0, 3, 4).reshape(2, 8, 64, 256)
    keep = lax.dynamic_index_in_dim(mixed_part, core_of, 0, keepdims=False)
    give = lax.dynamic_index_in_dim(mixed_part, 1 - core_of, 0, keepdims=False)
    mixed_half = keep + lax.ppermute(give, "gx", twin)
    mixed_half, gram = lax.optimization_barrier((mixed_half, gram))
    mixed = swap(mixed_half, "gx", [list(range(0, gx, 2)), list(range(1, gx, 2))])

    inv_one, placed = first_factor(row.astype(jnp.int32)[None], gram)
    basis_one = jnp.einsum("it,st->is", first, inv_one, precision=HI)
    out = second_sketch(mixed, inv_one, placed, near, far)
    left = swap(out, "gx").reshape(128, 384)

    both_part = lax.dot_general(left[:, :256], left, (((0,), (0,)), ((), ())), precision=HI)
    both_own = sum_scatter(both_part.reshape(gy, 8, 384), "gy")
    gram_two = spread(both_own[:, :256], "gy").reshape(256, 256)
    core_own, gram_two = lax.optimization_barrier((both_own[:, 256:], gram_two))
    core_in = spread(core_own, "gy").reshape(256, 128)
    inv_two, basis_two = second_factor(gram_two, left)
    mine = lax.dynamic_slice_in_dim(inv_two, 8 * col, 8, 0)
    core = jnp.dot(mine, core_in, precision=HI).reshape(8, 8, 16)
    return (basis_one, basis_two, jnp.transpose(core, (2, 0, 1)))


def solution(mesh):
    in_specs = (P("gx", "gy", None), P("gy", None, None), P("gx", None, None))
    out_specs = (P("gx", None), P("gy", None), P("gx", "gy", None))
    return jax.shard_map(local, mesh=mesh, in_specs=in_specs, out_specs=out_specs, check_vma=False)
```

```python
import jax
import jax.numpy as jnp
from jax import lax
from jax.experimental import pallas as pl
from jax.experimental.pallas import tpu as pltpu
from jax.sharding import PartitionSpec as P

HI = lax.Precision.HIGHEST
H = 128


def spread_col(x,p):
    return jnp.broadcast_to(x[:,p:p+1],(8,H))


def spread_row(x,r):
    return jnp.broadcast_to(x[r:r+1,:],(8,H))


def eliminate(d_ref,e_ref,x_ref):
    sub=lax.broadcasted_iota(jnp.int32,(8,H),0)
    lane=lax.broadcasted_iota(jnp.int32,(8,H),1)
    for k in range(16):
        rows=slice(8*k,8*k+8)
        block=(lane>=8*k)&(lane<8*k+8)
        Dk=d_ref[rows,:]; Ek=e_ref[rows,:]
        cb=[spread_col(Dk,8*k+t) for t in range(8)]
        s=[[spread_row(cb[t],q) for t in range(q+1)] for q in range(8)]
        Dm=jnp.where(block,jnp.where(lane==8*k+sub,1.0,0.0),Dk)
        rD=[spread_row(Dm,t) for t in range(8)]
        rE=[spread_row(Ek,t) for t in range(8)]
        inv=[None]*8; f=[[None]*8 for _ in range(8)]; W=[[None]*8 for _ in range(8)]
        dsel=s[0][0]
        for j in range(8):
            inv[j]=1.0/s[j][j]
            if j: dsel=jnp.where(sub==j,s[j][j],dsel)
            for q in range(j+1,8):
                f[q][j]=s[q][j]*inv[j]
            for q in range(j+1,8):
                for t in range(j+1,q+1):
                    s[q][t]=s[q][t]-f[q][j]*s[t][j]
        for q in range(8):
            for t in range(q):
                a=f[q][t]
                for m in range(t+1,q):
                    a=a+f[q][m]*W[m][t]
                W[q][t]=-a
        uD=list(rD); uE=list(rE)
        for q in range(1,8):
            for t in range(q):
                uD[q]=uD[q]+W[q][t]*rD[t]
                uE[q]=uE[q]+W[q][t]*rE[t]
        for g in range(k+1,16):
            gr=slice(8*g,8*g+8)
            Dg=d_ref[gr,:]; Eg=e_ref[gr,:]
            c=[spread_col(Dg,8*k+t) for t in range(8)]
            Dg=jnp.where(block,0.0,Dg)
            for j in range(8):
                a=c[j]
                for t in range(j):
                    a=a+W[j][t]*c[t]
                a=a*inv[j]
                Dg=Dg-a*uD[j]; Eg=Eg-a*uE[j]
            d_ref[gr,:]=Dg; e_ref[gr,:]=Eg
        rs=1.0/jnp.sqrt(dsel)
        nD=uD[0]; nE=uE[0]
        for q in range(1,8):
            nD=jnp.where(sub==q,uD[q],nD); nE=jnp.where(sub==q,uE[q],nE)
        row=8*k+sub
        x_ref[rows,:]=jnp.where(lane<=row,nD,0.0)*rs
        e_ref[rows,:]=nE*rs


def dot0(a,b):
    return lax.dot_general(a,b,(((0,),(0,)),((),())),precision=HI,preferred_element_type=jnp.float32)


def dot_t(a, b):
    return lax.dot_general(a, b, (((1,), (1,)), ((), ())), precision=HI, preferred_element_type=jnp.float32)


def factor_rows(g_ref, o_ref, d_ref, e_ref, x_ref):
    d_ref[...] = g_ref[:H, :H]
    e_ref[...] = g_ref[:H, H : 2 * H]

    def body(b, carry):
        eliminate(d_ref, e_ref, x_ref)

        @pl.when(b == 0)
        def _():
            o_ref[:H, :H] = x_ref[...]
            o_ref[:H, H:] = jnp.zeros((H, H), jnp.float32)
            u = e_ref[...]
            d_ref[...] = g_ref[H:, H : 2 * H] - dot0(u, u)
            e_ref[...] = -dot0(u, x_ref[...])

        return carry

    lax.fori_loop(0, 2, body, 0)
    o_ref[H:, H:] = x_ref[...]
    o_ref[H:, :H] = e_ref[...]


def first_factor_kernel(i_ref, g_ref, o_ref, p_ref, d_ref, e_ref, x_ref):
    factor_rows(g_ref, o_ref, d_ref, e_ref, x_ref)
    me = i_ref[0]
    y, c = me >> 1, me & 1
    for b in range(16):
        their_y, their_c = b // 2, b % 2
        step = (y - their_y) if their_c == 0 else (their_y - y)
        turned = ((step & 1) << 2) | (step & 2) | ((step >> 2) & 1)
        place = 8 * (c ^ their_c) + turned
        p_ref[pl.ds(pl.multiple_of(16 * place, 16), 16), :] = o_ref[16 * b : 16 * b + 16, :]


def second_factor_kernel(i_ref, g_ref, left_ref, b_ref, c_ref, o_ref, d_ref, e_ref, x_ref):
    factor_rows(g_ref, o_ref, d_ref, e_ref, x_ref)
    b_ref[...] = dot_t(left_ref[:, :256], o_ref[...])
    mine = o_ref[pl.ds(pl.multiple_of(8 * i_ref[0], 8), 8), :]
    core = jnp.dot(mine, g_ref[:, 256:], precision=HI, preferred_element_type=jnp.float32)
    for k in range(8):
        c_ref[:, k, :] = core[:, 16 * k : 16 * k + 16]


def second_sketch_kernel(m_ref, x_ref, p_ref, s_ref, t_ref, o_ref):
    mixed = m_ref[0]
    for i in range(1, 4):
        mixed = mixed + m_ref[i]
    placed = dot_t(mixed, p_ref[...])
    second = jnp.zeros((8, 256), jnp.float32)
    for k in range(8):
        rows = placed[8 * k : 8 * k + 8]
        for half, ref in enumerate((s_ref, t_ref)):
            block = ref[:, k].reshape(H, 256)
            second = second + jnp.dot(
                rows[:, H * half : H * half + H], block, precision=HI, preferred_element_type=jnp.float32
            )
    core = dot_t(mixed, x_ref[...])
    lane = lax.broadcasted_iota(jnp.int32, (8, H), 1)
    for m in range(16):
        chunk = jnp.zeros((8, H), jnp.float32)
        for k in range(8):
            half = core[8 * k : 8 * k + 8, H * (m // 8) : H * (m // 8) + H]
            shift = (16 * (k - m % 8)) % H
            moved = pltpu.roll(half, shift, 1) if shift else half
            chunk = jnp.where((lane >= 16 * k) & (lane < 16 * k + 16), moved, chunk)
        o_ref[m, :, :256] = second
        o_ref[m, :, 256:] = chunk


VMEM = pl.BlockSpec(memory_space=pltpu.VMEM)
SMEM = pl.BlockSpec(memory_space=pltpu.SMEM)
SQUARE = jax.ShapeDtypeStruct((256, 256), jnp.float32)
SCRATCH = [pltpu.VMEM((H, H), jnp.float32)] * 3
FACTOR_COST = pl.CostEstimate(flops=6_000_000_000, bytes_accessed=786432, transcendentals=0)


def first_factor(index, gram):
    return pl.pallas_call(
        first_factor_kernel,
        out_shape=(SQUARE, SQUARE),
        in_specs=[SMEM, VMEM],
        out_specs=(VMEM, VMEM),
        scratch_shapes=SCRATCH,
        cost_estimate=FACTOR_COST,
        compiler_params=pltpu.CompilerParams(vmem_limit_bytes=4 << 20),
        name="first_factor",
    )(index, gram)


def second_factor(index, gram, left):
    return pl.pallas_call(
        second_factor_kernel,
        out_shape=(jax.ShapeDtypeStruct((128, 256), jnp.float32), jax.ShapeDtypeStruct((8, 8, 16), jnp.float32)),
        in_specs=[SMEM, VMEM, VMEM],
        out_specs=(VMEM, VMEM),
        scratch_shapes=[pltpu.VMEM((256, 256), jnp.float32)] + SCRATCH,
        cost_estimate=FACTOR_COST,
        compiler_params=pltpu.CompilerParams(vmem_limit_bytes=4 << 20),
        name="second_factor",
    )(index, gram, left)


def second_sketch(mixed, inverse, placed, near, far):
    return pl.pallas_call(
        second_sketch_kernel,
        out_shape=jax.ShapeDtypeStruct((16, 8, 384), jnp.float32),
        in_specs=[VMEM] * 5,
        out_specs=VMEM,
        cost_estimate=pl.CostEstimate(flops=200_000_000, bytes_accessed=4_000_000, transcendentals=0),
        compiler_params=pltpu.CompilerParams(vmem_limit_bytes=12 << 20),
        name="second_sketch",
    )(mixed, inverse, placed, near, far)


def swap(pieces, axis, groups=None):
    return lax.all_to_all(pieces, axis, 0, 0, axis_index_groups=groups, tiled=True)


def sum_scatter(pieces, axis):
    return swap(pieces, axis).sum(0)


def spread(piece, axis):
    return swap(jnp.broadcast_to(piece[None], (lax.axis_size(axis),) + piece.shape), axis)


def local(tensor, sketch_one, sketch_two):
    gx, gy = 16, 32
    row, col = lax.axis_index("gx"), lax.axis_index("gy")

    def turn(d):
        return [(2 * y + c, 2 * ((y + (d if c == 0 else -d)) % 8) + c) for y in range(8) for c in range(2)]

    near = jnp.swapaxes(sketch_two, 0, 1)[None]
    for d in (4, 2, 1):
        near = jnp.concatenate([near, lax.ppermute(near, "gx", turn(d))], axis=0)
    far = lax.ppermute(near, "gx", [(i, i ^ 1) for i in range(gx)])

    part = jnp.einsum("ijk,jkc->ic", tensor, sketch_one, precision=HI)
    first_own = sum_scatter(part.reshape(gy, 8, 256), "gy")
    first = spread(first_own, "gy").reshape(256, 256)

    gram_part = lax.dot_general(first, first, (((0,), (0,)), ((), ())), precision=HI)
    gram_own = spread(lax.dynamic_slice_in_dim(gram_part, 8 * col, 8, 0), "gx").sum(0)
    gram = spread(gram_own, "gy").reshape(256, 256)

    mixed_part = jnp.einsum("ijk,ir->kjr", tensor, first, precision=HI)
    mixed_part = mixed_part.reshape(8, 4, 2, 2, 8, 256).transpose(3, 2, 1, 0, 4, 5).reshape(2, 2, 4, 64, 256)
    for bit, here in ((1, row % 2), (2, (row // 2) % 2)):
        keep = lax.dynamic_index_in_dim(mixed_part, here, 0, keepdims=False)
        give = lax.dynamic_index_in_dim(mixed_part, 1 - here, 0, keepdims=False)
        mixed_part = keep + lax.ppermute(give, "gx", [(i, i ^ bit) for i in range(gx)])
    mixed_part, gram = lax.optimization_barrier((mixed_part, gram))
    mixed = swap(mixed_part, "gx", [list(range(i, gx, 4)) for i in range(4)])

    inv_one, placed = first_factor(row.astype(jnp.int32)[None], gram)
    basis_one = jnp.einsum("it,st->is", first, inv_one, precision=HI)
    out = second_sketch(mixed, inv_one, placed, near, far)
    left = swap(out, "gx").reshape(128, 384)

    both_part = lax.dot_general(left[:, :256], left, (((0,), (0,)), ((), ())), precision=HI)
    both_own = sum_scatter(both_part.reshape(gy, 8, 384), "gy")
    both = spread(both_own, "gy").reshape(256, 384)
    basis_two, core = second_factor(col.astype(jnp.int32)[None], both, left)
    return (basis_one, basis_two, jnp.transpose(core, (2, 0, 1)))


def solution(mesh):
    in_specs = (P("gx", "gy", None), P("gy", None, None), P("gx", None, None))
    out_specs = (P("gx", None), P("gy", None), P("gx", "gy", None))
    return jax.shard_map(local, mesh=mesh, in_specs=in_specs, out_specs=out_specs, check_vma=False)
```

```python
import jax
import jax.numpy as jnp
from jax import lax
from jax.experimental import pallas as pl
from jax.experimental.pallas import tpu as pltpu
from jax.sharding import PartitionSpec as P

HI = lax.Precision.HIGHEST
H = 128


def spread_col(x,p):
    return jnp.broadcast_to(x[:,p:p+1],(8,H))


def spread_row(x,r):
    return jnp.broadcast_to(x[r:r+1,:],(8,H))


def eliminate(d_ref,e_ref,x_ref):
    sub=lax.broadcasted_iota(jnp.int32,(8,H),0)
    lane=lax.broadcasted_iota(jnp.int32,(8,H),1)
    left=[]; right=[]
    for k in range(16):
        rows=slice(8*k,8*k+8)
        block=(lane>=8*k)&(lane<8*k+8)
        Dk=d_ref[rows,:]; Ek=e_ref[rows,:]
        cb=[spread_col(Dk,8*k+t) for t in range(8)]
        s=[[spread_row(cb[t],q) for t in range(q+1)] for q in range(8)]
        Dm=jnp.where(block,jnp.where(lane==8*k+sub,1.0,0.0),Dk)
        rD=[spread_row(Dm,t) for t in range(8)]
        rE=[spread_row(Ek,t) for t in range(8)]
        inv=[None]*8; f=[[None]*8 for _ in range(8)]; W=[[None]*8 for _ in range(8)]
        dsel=s[0][0]
        for j in range(8):
            inv[j]=1.0/s[j][j]
            if j: dsel=jnp.where(sub==j,s[j][j],dsel)
            for q in range(j+1,8):
                f[q][j]=s[q][j]*inv[j]
            for q in range(j+1,8):
                for t in range(j+1,q+1):
                    s[q][t]=s[q][t]-f[q][j]*s[t][j]
        for q in range(8):
            for t in range(q):
                a=f[q][t]
                for m in range(t+1,q):
                    a=a+f[q][m]*W[m][t]
                W[q][t]=-a
        uD=list(rD); uE=list(rE)
        for q in range(1,8):
            for t in range(q):
                uD[q]=uD[q]+W[q][t]*rD[t]
                uE[q]=uE[q]+W[q][t]*rE[t]
        for g in range(k+1,min(16,(k//8+1)*8)):
            gr=slice(8*g,8*g+8)
            Dg=d_ref[gr,:]; Eg=e_ref[gr,:]
            c=[spread_col(Dg,8*k+t) for t in range(8)]
            Dg=jnp.where(block,0.0,Dg)
            for j in range(8):
                a=c[j]
                for t in range(j):
                    a=a+W[j][t]*c[t]
                a=a*inv[j]
                Dg=Dg-a*uD[j]; Eg=Eg-a*uE[j]
            d_ref[gr,:]=Dg; e_ref[gr,:]=Eg
        rs=1.0/jnp.sqrt(dsel)
        nD=uD[0]; nE=uE[0]; isel=inv[0]
        for q in range(1,8):
            nD=jnp.where(sub==q,uD[q],nD); nE=jnp.where(sub==q,uE[q],nE); isel=jnp.where(sub==q,inv[q],isel)
        row=8*k+sub
        x_ref[rows,:]=jnp.where(lane<=row,nD,0.0)*rs
        e_ref[rows,:]=nE*rs
        end=8*8*(k//8+1)
        left.append(nD*isel)
        right.append(jnp.concatenate([jnp.where((lane<=row)|(lane>=end),nD,0.0),nE],axis=1))
        if k%8==8-1 and k<15:
            upd=dot0(jnp.concatenate(left,axis=0),jnp.concatenate(right,axis=0))
            left=[]; right=[]
            inblk=(lane>=end-8*8)&(lane<end)
            for g in range(k+1,16):
                gr=slice(8*g,8*g+8)
                d_ref[gr,:]=jnp.where(inblk,0.0,d_ref[gr,:])-upd[gr,:H]
                e_ref[gr,:]=e_ref[gr,:]-upd[gr,H:]


def dot0(a,b):
    return lax.dot_general(a,b,(((0,),(0,)),((),())),precision=HI,preferred_element_type=jnp.float32)


def dot_t(a, b):
    return lax.dot_general(a, b, (((1,), (1,)), ((), ())), precision=HI, preferred_element_type=jnp.float32)


def factor_rows(g_ref, o_ref, d_ref, e_ref, x_ref):
    d_ref[...] = g_ref[:H, :H]
    e_ref[...] = g_ref[:H, H : 2 * H]

    def body(b, carry):
        eliminate(d_ref, e_ref, x_ref)

        @pl.when(b == 0)
        def _():
            o_ref[:H, :H] = x_ref[...]
            o_ref[:H, H:] = jnp.zeros((H, H), jnp.float32)
            u = e_ref[...]
            d_ref[...] = g_ref[H:, H : 2 * H] - dot0(u, u)
            e_ref[...] = -dot0(u, x_ref[...])

        return carry

    lax.fori_loop(0, 2, body, 0)
    o_ref[H:, H:] = x_ref[...]
    o_ref[H:, :H] = e_ref[...]


def first_dot_kernel(a_ref, s_ref, o_ref):
    total = jnp.zeros((256, 256), jnp.float32)
    for k in range(0, 8, 2):
        cells = jnp.concatenate([a_ref[:, k, :], a_ref[:, k + 1, :]], axis=1)
        test = jnp.concatenate([s_ref[:, k, :], s_ref[:, k + 1, :]], axis=0)
        total = total + jnp.dot(cells, test, precision=HI, preferred_element_type=jnp.float32)
    o_ref[...] = total


def first_factor_kernel(i_ref, g_ref, o_ref, p_ref, d_ref, e_ref, x_ref):
    factor_rows(g_ref, o_ref, d_ref, e_ref, x_ref)
    me = i_ref[0]
    y, c = me >> 1, me & 1
    for b in range(16):
        their_y, their_c = b // 2, b % 2
        step = (y - their_y) if their_c == 0 else (their_y - y)
        turned = ((step & 1) << 2) | (step & 2) | ((step >> 2) & 1)
        place = 8 * (c ^ their_c) + turned
        p_ref[pl.ds(pl.multiple_of(16 * place, 16), 16), :] = o_ref[16 * b : 16 * b + 16, :]


def second_factor_kernel(i_ref, g_ref, left_ref, b_ref, c_ref, o_ref, d_ref, e_ref, x_ref):
    factor_rows(g_ref, o_ref, d_ref, e_ref, x_ref)
    b_ref[...] = dot_t(left_ref[:, :256], o_ref[...])
    mine = o_ref[pl.ds(pl.multiple_of(8 * i_ref[0], 8), 8), :]
    core = jnp.dot(mine, g_ref[:, 256:], precision=HI, preferred_element_type=jnp.float32)
    for k in range(8):
        c_ref[:, k, :] = core[:, 16 * k : 16 * k + 16]


def second_sketch_kernel(m_ref, x_ref, p_ref, s_ref, t_ref, o_ref):
    mixed = m_ref[0]
    for i in range(1, 4):
        mixed = mixed + m_ref[i]
    placed = dot_t(mixed, p_ref[...])
    second = jnp.zeros((8, 256), jnp.float32)
    for k in range(8):
        rows = placed[8 * k : 8 * k + 8]
        for half, ref in enumerate((s_ref, t_ref)):
            block = ref[:, k].reshape(H, 256)
            second = second + jnp.dot(
                rows[:, H * half : H * half + H], block, precision=HI, preferred_element_type=jnp.float32
            )
    core = dot_t(mixed, x_ref[...])
    lane = lax.broadcasted_iota(jnp.int32, (8, H), 1)
    for m in range(16):
        chunk = jnp.zeros((8, H), jnp.float32)
        for k in range(8):
            half = core[8 * k : 8 * k + 8, H * (m // 8) : H * (m // 8) + H]
            shift = (16 * (k - m % 8)) % H
            moved = pltpu.roll(half, shift, 1) if shift else half
            chunk = jnp.where((lane >= 16 * k) & (lane < 16 * k + 16), moved, chunk)
        o_ref[m, :, :256] = second
        o_ref[m, :, 256:] = chunk


GRANT = 5 << 20
VMEM = pl.BlockSpec(memory_space=pltpu.VMEM)
SMEM = pl.BlockSpec(memory_space=pltpu.SMEM)
SQUARE = jax.ShapeDtypeStruct((256, 256), jnp.float32)
SCRATCH = [pltpu.VMEM((H, H), jnp.float32)] * 3
FACTOR_COST = pl.CostEstimate(flops=6_000_000_000, bytes_accessed=786432, transcendentals=0)


def first_dot(cells, test):
    return pl.pallas_call(
        first_dot_kernel,
        out_shape=SQUARE,
        in_specs=[VMEM, VMEM],
        out_specs=VMEM,
        cost_estimate=pl.CostEstimate(flops=800_000_000, bytes_accessed=2_500_000, transcendentals=0),
        compiler_params=pltpu.CompilerParams(vmem_limit_bytes=GRANT),
        name="first_dot",
    )(cells, test)


def first_factor(index, gram):
    return pl.pallas_call(
        first_factor_kernel,
        out_shape=(SQUARE, SQUARE),
        in_specs=[SMEM, VMEM],
        out_specs=(VMEM, VMEM),
        scratch_shapes=SCRATCH,
        cost_estimate=FACTOR_COST,
        compiler_params=pltpu.CompilerParams(vmem_limit_bytes=GRANT),
        name="first_factor",
    )(index, gram)


def second_factor(index, gram, left):
    return pl.pallas_call(
        second_factor_kernel,
        out_shape=(jax.ShapeDtypeStruct((128, 256), jnp.float32), jax.ShapeDtypeStruct((8, 8, 16), jnp.float32)),
        in_specs=[SMEM, VMEM, VMEM],
        out_specs=(VMEM, VMEM),
        scratch_shapes=[pltpu.VMEM((256, 256), jnp.float32)] + SCRATCH,
        cost_estimate=FACTOR_COST,
        compiler_params=pltpu.CompilerParams(vmem_limit_bytes=GRANT),
        name="second_factor",
    )(index, gram, left)


def second_sketch(mixed, inverse, placed, near, far):
    return pl.pallas_call(
        second_sketch_kernel,
        out_shape=jax.ShapeDtypeStruct((16, 8, 384), jnp.float32),
        in_specs=[VMEM] * 5,
        out_specs=VMEM,
        cost_estimate=pl.CostEstimate(flops=200_000_000, bytes_accessed=4_000_000, transcendentals=0),
        compiler_params=pltpu.CompilerParams(vmem_limit_bytes=GRANT),
        name="second_sketch",
    )(mixed, inverse, placed, near, far)


def swap(pieces, axis, groups=None):
    return lax.all_to_all(pieces, axis, 0, 0, axis_index_groups=groups, tiled=True)


def sum_scatter(pieces, axis):
    return swap(pieces, axis).sum(0)


def spread(piece, axis):
    return swap(jnp.broadcast_to(piece[None], (lax.axis_size(axis),) + piece.shape), axis)


def local(tensor, sketch_one, sketch_two):
    gx, gy = 16, 32
    row, col = lax.axis_index("gx"), lax.axis_index("gy")

    def turn(d):
        return [(2 * y + c, 2 * ((y + (d if c == 0 else -d)) % 8) + c) for y in range(8) for c in range(2)]

    near = jnp.swapaxes(sketch_two, 0, 1)[None]
    for d in (4, 2, 1):
        near = jnp.concatenate([near, lax.ppermute(near, "gx", turn(d))], axis=0)
    far = lax.ppermute(near, "gx", [(i, i ^ 1) for i in range(gx)])

    part = first_dot(jnp.swapaxes(tensor, 1, 2), sketch_one)
    first_own = sum_scatter(part.reshape(gy, 8, 256), "gy")
    first = spread(first_own, "gy").reshape(256, 256)

    gram_part = lax.dot_general(first, first, (((0,), (0,)), ((), ())), precision=HI)
    gram_own = spread(lax.dynamic_slice_in_dim(gram_part, 8 * col, 8, 0), "gx").sum(0)
    gram = spread(gram_own, "gy").reshape(256, 256)

    mixed_part = jnp.einsum("ijk,ir->kjr", tensor, first, precision=HI)
    mixed_part = mixed_part.reshape(8, 4, 2, 2, 8, 256).transpose(3, 2, 1, 0, 4, 5).reshape(2, 2, 4, 64, 256)
    for bit, here in ((1, row % 2), (2, (row // 2) % 2)):
        keep = lax.dynamic_index_in_dim(mixed_part, here, 0, keepdims=False)
        give = lax.dynamic_index_in_dim(mixed_part, 1 - here, 0, keepdims=False)
        mixed_part = keep + lax.ppermute(give, "gx", [(i, i ^ bit) for i in range(gx)])
    mixed = swap(mixed_part, "gx", [list(range(i, gx, 4)) for i in range(4)])

    inv_one, placed = first_factor(row.astype(jnp.int32)[None], gram)
    basis_one = jnp.einsum("it,st->is", first, inv_one, precision=HI)
    out = second_sketch(mixed, inv_one, placed, near, far)
    left = swap(out, "gx").reshape(128, 384)

    both_part = lax.dot_general(left[:, :256], left, (((0,), (0,)), ((), ())), precision=HI)
    both_own = sum_scatter(both_part.reshape(gy, 8, 384), "gy")
    both = spread(both_own, "gy").reshape(256, 384)
    basis_two, core = second_factor(col.astype(jnp.int32)[None], both, left)
    return (basis_one, basis_two, jnp.transpose(core, (2, 0, 1)))


def solution(mesh):
    in_specs = (P("gx", "gy", None), P("gy", None, None), P("gx", None, None))
    out_specs = (P("gx", None), P("gy", None), P("gx", "gy", None))
    return jax.shard_map(local, mesh=mesh, in_specs=in_specs, out_specs=out_specs, check_vma=False)
```

```python
import jax
import jax.numpy as jnp
from jax import lax
from jax.experimental import pallas as pl
from jax.experimental.pallas import tpu as pltpu
from jax.sharding import PartitionSpec as P

HI = lax.Precision.HIGHEST
H = 128


def spread_col(x,p):
    return jnp.broadcast_to(x[:,p:p+1],(8,H))


def spread_row(x,r):
    return jnp.broadcast_to(x[r:r+1,:],(8,H))


def eliminate(d_ref,e_ref,x_ref):
    sub=lax.broadcasted_iota(jnp.int32,(8,H),0)
    lane=lax.broadcasted_iota(jnp.int32,(8,H),1)
    left=[]; right=[]
    for k in range(16):
        rows=slice(8*k,8*k+8)
        block=(lane>=8*k)&(lane<8*k+8)
        Dk=d_ref[rows,:]; Ek=e_ref[rows,:]
        cb=[spread_col(Dk,8*k+t) for t in range(8)]
        s=[[spread_row(cb[t],q) for t in range(q+1)] for q in range(8)]
        Dm=jnp.where(block,jnp.where(lane==8*k+sub,1.0,0.0),Dk)
        rD=[spread_row(Dm,t) for t in range(8)]
        rE=[spread_row(Ek,t) for t in range(8)]
        inv=[None]*8; f=[[None]*8 for _ in range(8)]; W=[[None]*8 for _ in range(8)]
        dsel=s[0][0]
        for j in range(8):
            inv[j]=1.0/s[j][j]
            if j: dsel=jnp.where(sub==j,s[j][j],dsel)
            for q in range(j+1,8):
                f[q][j]=s[q][j]*inv[j]
            for q in range(j+1,8):
                for t in range(j+1,q+1):
                    s[q][t]=s[q][t]-f[q][j]*s[t][j]
        for q in range(8):
            for t in range(q):
                a=f[q][t]
                for m in range(t+1,q):
                    a=a+f[q][m]*W[m][t]
                W[q][t]=-a
        uD=list(rD); uE=list(rE)
        for q in range(1,8):
            for t in range(q):
                uD[q]=uD[q]+W[q][t]*rD[t]
                uE[q]=uE[q]+W[q][t]*rE[t]
        for g in range(k+1,min(16,(k//8+1)*8)):
            gr=slice(8*g,8*g+8)
            Dg=d_ref[gr,:]; Eg=e_ref[gr,:]
            c=[spread_col(Dg,8*k+t) for t in range(8)]
            Dg=jnp.where(block,0.0,Dg)
            for j in range(8):
                a=c[j]
                for t in range(j):
                    a=a+W[j][t]*c[t]
                a=a*inv[j]
                Dg=Dg-a*uD[j]; Eg=Eg-a*uE[j]
            d_ref[gr,:]=Dg; e_ref[gr,:]=Eg
        rs=1.0/jnp.sqrt(dsel)
        nD=uD[0]; nE=uE[0]; isel=inv[0]
        for q in range(1,8):
            nD=jnp.where(sub==q,uD[q],nD); nE=jnp.where(sub==q,uE[q],nE); isel=jnp.where(sub==q,inv[q],isel)
        row=8*k+sub
        x_ref[rows,:]=jnp.where(lane<=row,nD,0.0)*rs
        e_ref[rows,:]=nE*rs
        end=8*8*(k//8+1)
        left.append(nD*isel)
        right.append(jnp.concatenate([jnp.where((lane<=row)|(lane>=end),nD,0.0),nE],axis=1))
        if k%8==8-1 and k<15:
            upd=dot0(jnp.concatenate(left,axis=0),jnp.concatenate(right,axis=0))
            left=[]; right=[]
            inblk=(lane>=end-8*8)&(lane<end)
            for g in range(k+1,16):
                gr=slice(8*g,8*g+8)
                d_ref[gr,:]=jnp.where(inblk,0.0,d_ref[gr,:])-upd[gr,:H]
                e_ref[gr,:]=e_ref[gr,:]-upd[gr,H:]


def dot0(a,b):
    return lax.dot_general(a,b,(((0,),(0,)),((),())),precision=HI,preferred_element_type=jnp.float32)


def dot_t(a, b):
    return lax.dot_general(a, b, (((1,), (1,)), ((), ())), precision=HI, preferred_element_type=jnp.float32)


def factor_rows(g_ref, o_ref, d_ref, e_ref, x_ref):
    d_ref[...] = g_ref[:H, :H]
    e_ref[...] = g_ref[:H, H : 2 * H]

    def body(b, carry):
        eliminate(d_ref, e_ref, x_ref)

        @pl.when(b == 0)
        def _():
            o_ref[:H, :H] = x_ref[...]
            o_ref[:H, H:] = jnp.zeros((H, H), jnp.float32)
            u = e_ref[...]
            d_ref[...] = g_ref[H:, H : 2 * H] - dot0(u, u)
            e_ref[...] = -dot0(u, x_ref[...])

        return carry

    lax.fori_loop(0, 2, body, 0)
    o_ref[H:, H:] = x_ref[...]
    o_ref[H:, :H] = e_ref[...]


def first_dot_kernel(a_ref, s_ref, o_ref):
    total = jnp.zeros((256, 256), jnp.float32)
    for k in range(0, 8, 2):
        cells = jnp.concatenate([a_ref[:, k, :], a_ref[:, k + 1, :]], axis=1)
        test = jnp.concatenate([s_ref[:, k, :], s_ref[:, k + 1, :]], axis=0)
        total = total + jnp.dot(cells, test, precision=HI, preferred_element_type=jnp.float32)
    o_ref[...] = total


def first_factor_kernel(i_ref, g_ref, o_ref, p_ref, d_ref, e_ref, x_ref):
    factor_rows(g_ref, o_ref, d_ref, e_ref, x_ref)
    me = i_ref[0]
    y, c = me >> 1, me & 1
    for b in range(16):
        their_y, their_c = b // 2, b % 2
        step = (y - their_y) if their_c == 0 else (their_y - y)
        turned = ((step & 1) << 2) | (step & 2) | ((step >> 2) & 1)
        place = 8 * (c ^ their_c) + turned
        p_ref[pl.ds(pl.multiple_of(16 * place, 16), 16), :] = o_ref[16 * b : 16 * b + 16, :]


def second_factor_kernel(i_ref, g_ref, left_ref, b_ref, c_ref, o_ref, d_ref, e_ref, x_ref):
    factor_rows(g_ref, o_ref, d_ref, e_ref, x_ref)
    b_ref[...] = dot_t(left_ref[:, :256], o_ref[...])
    mine = o_ref[pl.ds(pl.multiple_of(8 * i_ref[0], 8), 8), :]
    core = jnp.dot(mine, g_ref[:, 256:], precision=HI, preferred_element_type=jnp.float32)
    for k in range(8):
        c_ref[:, k, :] = core[:, 16 * k : 16 * k + 16]


def second_sketch_kernel(m_ref, x_ref, p_ref, s_ref, t_ref, o_ref):
    mixed = m_ref[0]
    for i in range(1, 4):
        mixed = mixed + m_ref[i]
    placed = dot_t(mixed, p_ref[...])
    second = jnp.zeros((8, 256), jnp.float32)
    for k in range(8):
        rows = placed[8 * k : 8 * k + 8]
        for half, ref in enumerate((s_ref, t_ref)):
            block = ref[:, k].reshape(H, 256)
            second = second + jnp.dot(
                rows[:, H * half : H * half + H], block, precision=HI, preferred_element_type=jnp.float32
            )
    core = dot_t(mixed, x_ref[...])
    lane = lax.broadcasted_iota(jnp.int32, (8, H), 1)
    for m in range(16):
        chunk = jnp.zeros((8, H), jnp.float32)
        for k in range(8):
            half = core[8 * k : 8 * k + 8, H * (m // 8) : H * (m // 8) + H]
            shift = (16 * (k - m % 8)) % H
            moved = pltpu.roll(half, shift, 1) if shift else half
            chunk = jnp.where((lane >= 16 * k) & (lane < 16 * k + 16), moved, chunk)
        o_ref[m, :, :256] = second
        o_ref[m, :, 256:] = chunk


GRANT = 5 << 20
VMEM = pl.BlockSpec(memory_space=pltpu.VMEM)
SMEM = pl.BlockSpec(memory_space=pltpu.SMEM)
SQUARE = jax.ShapeDtypeStruct((256, 256), jnp.float32)
SCRATCH = [pltpu.VMEM((H, H), jnp.float32)] * 3
FACTOR_COST = pl.CostEstimate(flops=6_000_000_000, bytes_accessed=786432, transcendentals=0)


def first_dot(cells, test):
    return pl.pallas_call(
        first_dot_kernel,
        out_shape=SQUARE,
        in_specs=[VMEM, VMEM],
        out_specs=VMEM,
        cost_estimate=pl.CostEstimate(flops=800_000_000, bytes_accessed=2_500_000, transcendentals=0),
        compiler_params=pltpu.CompilerParams(vmem_limit_bytes=GRANT),
        name="first_dot",
    )(cells, test)


def first_factor(index, gram):
    return pl.pallas_call(
        first_factor_kernel,
        out_shape=(SQUARE, SQUARE),
        in_specs=[SMEM, VMEM],
        out_specs=(VMEM, VMEM),
        scratch_shapes=SCRATCH,
        cost_estimate=FACTOR_COST,
        compiler_params=pltpu.CompilerParams(vmem_limit_bytes=GRANT),
        name="first_factor",
    )(index, gram)


def second_factor(index, gram, left):
    return pl.pallas_call(
        second_factor_kernel,
        out_shape=(jax.ShapeDtypeStruct((128, 256), jnp.float32), jax.ShapeDtypeStruct((8, 8, 16), jnp.float32)),
        in_specs=[SMEM, VMEM, VMEM],
        out_specs=(VMEM, VMEM),
        scratch_shapes=[pltpu.VMEM((256, 256), jnp.float32)] + SCRATCH,
        cost_estimate=FACTOR_COST,
        compiler_params=pltpu.CompilerParams(vmem_limit_bytes=GRANT),
        name="second_factor",
    )(index, gram, left)


def second_sketch(mixed, inverse, placed, near, far):
    return pl.pallas_call(
        second_sketch_kernel,
        out_shape=jax.ShapeDtypeStruct((16, 8, 384), jnp.float32),
        in_specs=[VMEM] * 5,
        out_specs=VMEM,
        cost_estimate=pl.CostEstimate(flops=200_000_000, bytes_accessed=4_000_000, transcendentals=0),
        compiler_params=pltpu.CompilerParams(vmem_limit_bytes=GRANT),
        name="second_sketch",
    )(mixed, inverse, placed, near, far)


def swap(pieces, axis, groups=None):
    return lax.all_to_all(pieces, axis, 0, 0, axis_index_groups=groups, tiled=True)


def sum_scatter(pieces, axis):
    return swap(pieces, axis).sum(0)


def spread(piece, axis):
    return swap(jnp.broadcast_to(piece[None], (lax.axis_size(axis),) + piece.shape), axis)


def local(tensor, sketch_one, sketch_two):
    gx, gy = 16, 32
    row, col = lax.axis_index("gx"), lax.axis_index("gy")

    def turn(d):
        return [(2 * y + c, 2 * ((y + (d if c == 0 else -d)) % 8) + c) for y in range(8) for c in range(2)]

    near = jnp.swapaxes(sketch_two, 0, 1)[None]
    for d in (4, 2, 1):
        near = jnp.concatenate([near, lax.ppermute(near, "gx", turn(d))], axis=0)
    far = lax.ppermute(near, "gx", [(i, i ^ 1) for i in range(gx)])

    part = first_dot(jnp.swapaxes(tensor, 1, 2), sketch_one)
    first_own = sum_scatter(part.reshape(gy, 8, 256), "gy")
    first = spread(first_own, "gy").reshape(256, 256)

    gram_part = lax.dot_general(first, first, (((0,), (0,)), ((), ())), precision=HI)
    gram_own = spread(lax.dynamic_slice_in_dim(gram_part, 8 * col, 8, 0), "gx").sum(0)
    gram = spread(gram_own, "gy").reshape(256, 256)

    mixed_part = jnp.einsum("ijk,ir->kjr", tensor, first, precision=HI)
    mixed_part = mixed_part.reshape(8, 4, 2, 2, 8, 256).transpose(3, 2, 1, 0, 4, 5).reshape(2, 2, 4, 64, 256)
    core_bit, chip_bit = row % 2, (row // 2) % 2

    def pick(block, bit):
        return lax.dynamic_index_in_dim(block, bit, 0, keepdims=False)

    mine = pick(mixed_part, core_bit)
    theirs = lax.ppermute(pick(mixed_part, 1 - core_bit), "gx", [(i, i ^ 1) for i in range(gx)])
    give = pick(mine, 1 - chip_bit) + pick(theirs, 1 - chip_bit)
    other = lax.ppermute(give, "gx", [(i, i ^ 2) for i in range(gx)])
    mixed_part = (pick(mine, chip_bit) + pick(theirs, chip_bit)) + other
    mixed = swap(mixed_part, "gx", [list(range(i, gx, 4)) for i in range(4)])

    inv_one, placed = first_factor(row.astype(jnp.int32)[None], gram)
    basis_one = jnp.einsum("it,st->is", first, inv_one, precision=HI)
    out = second_sketch(mixed, inv_one, placed, near, far)
    left = swap(out, "gx").reshape(128, 384)

    both_part = lax.dot_general(left[:, :256], left, (((0,), (0,)), ((), ())), precision=HI)
    both_own = sum_scatter(both_part.reshape(gy, 8, 384), "gy")
    both = spread(both_own, "gy").reshape(256, 384)
    basis_two, core = second_factor(col.astype(jnp.int32)[None], both, left)
    return (basis_one, basis_two, jnp.transpose(core, (2, 0, 1)))


def solution(mesh):
    in_specs = (P("gx", "gy", None), P("gy", None, None), P("gx", None, None))
    out_specs = (P("gx", None), P("gy", None), P("gx", "gy", None))
    return jax.shard_map(local, mesh=mesh, in_specs=in_specs, out_specs=out_specs, check_vma=False)
```
